256 devices in a mesh: groups: 2 (over z), dp: 64 (over y, x), mp: 2 (over core).
Axes of the slice: x: 8, y: 8, z: 2, core: 2. Of those that a mesh axis runs over, the one named last changes fastest.
The devices are a block of a 8x8x16 slice.
Arguments:
- tokens: bfloat16 [32768, 8192], P(('groups', 'dp'), 'mp'), parts along dimension 0, may hold values from -6 to 6
- queries: bfloat16 [32768, 8192], P(('groups', 'dp'), 'mp'), parts along dimension 0, may hold values from -384 to 384, as said below
- w_key: bfloat16 [8192, 1024], P('dp', 'mp'), may hold values from -0.0625 to 0.0625
- w_value: bfloat16 [8192, 1024], P('dp', 'mp'), may hold values from -0.0625 to 0.0625
- lengths: int32 [16, 16], P('groups'), parts along dimension 0, may hold values from 1 to 1920, 2048 in all within a row
Outputs:
- attended: bfloat16 [32768, 8192], P(('groups', 'dp'), 'mp'), parts along dimension 0
The draws below stay inside these ranges and needn't reach their ends.
There are 2 independent parts, one for each index of `groups`. The reference program is written for one: setup_inputs(seed, part) draws one part's arguments, and reference() takes and returns one part's arrays. A program takes and returns all parts, laid end to end along the dimension named above; an argument that names none is the same for every part. Nothing has to cross between parts.
Inputs may be any that keep to these rules, and one draw needn't show every extreme that they name: Real-valued queries.
All inputs are finite; a program needn't handle non-finite values.
Results may differ from the reference program's by a relative error of at most 0.0055.
The reference program's roundings to bfloat16 on the way count: a program that leaves them out, or rounds other values in their place, can miss the bound.
Values may be sent and summed in bfloat16 or wider, within the bound.
A program may use at most 128 MiB of HBM per device.

```python
import math
import jax
import jax.numpy as jnp
import numpy as np
from jax import lax

D = 8192
H = 64
KV = 8
DH = 128
ROW = 2048
SEQ_ROW = 16
KVW = 1024
MOST = 1920
TOKENS = 16384
ROWS = 8


def draw_queries(key, part):
    base = jax.random.normal(jax.random.fold_in(key, 11), (TOKENS, H * DH), jnp.float32)
    return jnp.clip(base, -384.0, 384.0).astype(jnp.bfloat16)


def level_of(stream_key, extent, cuts, least, high):
    def one(dim, shards_of):
        heights = jax.random.uniform(jax.random.fold_in(jax.random.fold_in(stream_key, 6), dim), (shards_of,), jnp.float32, least / len(cuts), high / len(cuts))
        return jnp.repeat(jnp.exp(heights), extent[dim] // shards_of).reshape((-1,) + (1,) * (len(extent) - dim - 1))

    loudness = one(*cuts[0])
    for cut in cuts[1:]:
        loudness = loudness * one(*cut)
    return loudness


def length_profile(amount, total, limit, lean):
    weights = [(1 << 20) // math.isqrt(rank ** lean) + 1 for rank in range(2, amount + 1)]
    rest, given = total - limit - (amount - 1), [1] * (amount - 1)
    while rest > 0:
        free = [i for i in range(amount - 1) if given[i] < limit]
        pool, budget = sum([weights[i] for i in free]), rest
        for i in free:
            addition = min(limit - given[i], max(1, budget * weights[i] // pool), rest)
            given[i] = given[i] + addition
            rest = rest - addition
    return np.array([limit] + given)


def uneven(key, count, total, limit, slope):
    if count == 2:
        one = jax.random.randint(key, (), max(1, total - limit), min(limit, total - 1) + 1)
        return jnp.stack([one, total - one])
    sizes = jnp.asarray(length_profile(count, total, limit, slope), jnp.int32)
    twos = (count - 1) // 2
    source_of, taker = sizes[1:1 + 2 * twos:2], sizes[2:2 + 2 * twos:2]
    margin = jnp.minimum(source_of - 1, limit - taker)
    shifted = jax.random.randint(jax.random.fold_in(key, 1), (twos,), 0, 1 << 20) % (margin + 1)
    sizes = sizes.at[1:1 + 2 * twos:2].set(source_of - shifted).at[2:2 + 2 * twos:2].set(taker + shifted)
    return sizes[jax.random.permutation(jax.random.fold_in(key, 2), count)]


def bell_draw(rng, extent, width, most, cuts=(), kind=jnp.bfloat16):
    array = width * jax.random.normal(rng, extent, jnp.float32)
    if cuts:
        array = array * level_of(rng, extent, cuts, -0.22, 0.18)
    return jnp.clip(array, -most, most).astype(kind)


def setup_inputs(seed: int = 0, part: int = 0) -> dict:
    key_list = jax.random.split(jax.random.key(seed), 6)
    own_keys = jax.random.split(jax.random.fold_in(key_list[5], part), 6)
    return {
        "tokens": bell_draw(own_keys[0], (TOKENS, D), 1.0, 6.0, ((0, 64), (1, 2))),
        "queries": draw_queries(jax.random.fold_in(jax.random.fold_in(key_list[5], part), 71), part),
        "w_key": bell_draw(key_list[2], (D, KVW), D ** -0.5, 0.0625, ((0, 64), (1, 2))),
        "w_value": bell_draw(key_list[3], (D, KVW), D ** -0.5, 0.0625, ((0, 64), (1, 2))),
        "lengths": jax.vmap(lambda own: uneven(own, SEQ_ROW, ROW, MOST, 2))(jax.random.split(own_keys[4], ROWS)).reshape((ROWS, SEQ_ROW)).astype(jnp.int32),
    }


def rotate(values, positions):
    half_dim = values.shape[-1] // 2
    frequency = jnp.power(500000.0, -2.0 * jnp.arange(half_dim, dtype=jnp.float32) / values.shape[-1])
    angles = positions.astype(jnp.float32)[:, None] * frequency[None, :]
    cosine = jnp.cos(angles)[:, None, :]
    sine_part = jnp.sin(angles)[:, None, :]
    first_half = values[..., :half_dim]
    second_half = values[..., half_dim:]
    return jnp.concatenate([first_half * cosine - second_half * sine_part, second_half * cosine + first_half * sine_part], axis=-1)

def sequence_tables(lengths):
    finish = jnp.cumsum(lengths, axis=1)
    offsets = jnp.arange(ROW, dtype=jnp.int32)
    before = finish[:, None, :] <= offsets[None, :, None]
    sequence = lax.optimization_barrier(jnp.sum(before.astype(jnp.int32), axis=2))
    started = lax.optimization_barrier(jnp.sum(jnp.where(before, lengths[:, None, :], 0), axis=2))
    return (sequence, offsets[None, :] - started)

def reference(tokens, queries, w_key, w_value, lengths):
    half_row = ROW // 2
    tokens_rows = jnp.roll(tokens, -half_row, axis=0)
    queries_rows = jnp.roll(queries, -half_row, axis=0)
    sequence, positions = sequence_tables(lengths)
    keys_raw = jnp.dot(tokens_rows, w_key, preferred_element_type=jnp.float32).reshape(TOKENS, KV, DH)
    keys_all = rotate(keys_raw, positions.reshape(TOKENS)).astype(jnp.bfloat16)
    values_all = jnp.dot(tokens_rows, w_value, preferred_element_type=jnp.float32).astype(jnp.bfloat16)
    group_size = H // KV
    scale_factor = 1.0 / math.sqrt(DH)
    query_rows = queries_rows.reshape(ROWS, ROW, KV, group_size, DH)
    key_rows = keys_all.reshape(ROWS, ROW, KV, DH)
    value_rows = values_all.reshape(ROWS, ROW, KV, DH)
    causal = jnp.arange(ROW, dtype=jnp.int32)[None, :] <= jnp.arange(ROW, dtype=jnp.int32)[:, None]

    def one_row(row_items):
        query_row, key_row, value_row, sequence_row = row_items
        scores = jnp.einsum('tkgd,ukd->kgtu', query_row.astype(jnp.float32), key_row.astype(jnp.float32)) * scale_factor
        allowed = causal & (sequence_row[:, None] == sequence_row[None, :])
        masked = jnp.where(allowed, scores, -1e+30)
        row_peak = lax.optimization_barrier(jnp.max(masked, axis=-1, keepdims=True))
        weights = jnp.where(allowed, jnp.exp(masked - row_peak), 0.0)
        probability = (weights / lax.optimization_barrier(jnp.sum(weights, axis=-1, keepdims=True))).astype(jnp.bfloat16)
        mixed_heads = jnp.einsum('kgtu,ukd->tkgd', probability.astype(jnp.float32), value_row.astype(jnp.float32))
        return mixed_heads.reshape(ROW, H * DH).astype(jnp.bfloat16)
    attended = lax.map(one_row, (query_rows, key_rows, value_rows, sequence))
    return jnp.roll(attended.reshape(TOKENS, H * DH), half_row, axis=0)
```

```python
import functools
import math

import jax
import jax.numpy as jnp
from jax import lax
from jax.experimental import pallas as pl
from jax.experimental.pallas import tpu as pltpu
from jax.sharding import PartitionSpec as P

DH = 128
ROW = 2048
MESH = pl.DeviceIdType.MESH
PLUS, MINUS = 0, 1


def remote(src, dst, send, recv, device):
    return pltpu.make_async_remote_copy(
        src_ref=src,
        dst_ref=dst,
        send_sem=send,
        recv_sem=recv,
        device_id=device,
        device_id_type=MESH,
    )


def meet(neighbours):
    barrier = pltpu.get_barrier_semaphore()
    for device in neighbours:
        pl.semaphore_signal(barrier, inc=1, device_id=device, device_id_type=MESH)
    pl.semaphore_wait(barrier, len(neighbours))


def turned(x, table):
    half = DH // 2
    lane = lax.broadcasted_iota(jnp.int32, table.shape, 1)
    other = pltpu.roll(table, half, 1)
    cosine = jnp.where(lane < half, table, other)
    sine = jnp.where(lane < half, -other, table)
    return x * cosine + pltpu.roll(x, half, 1) * sine


def project_kernel(
    side, tokens, weight, table, kv, tok, w_all, tab, acc, give, got, local_sem,
    one_send, one_recv, two_send, two_recv, sib_send, sib_recv, z_send, z_recv,
):
    g, d, m = lax.axis_index("groups"), lax.axis_index("dp"), lax.axis_index("mp")
    x, y = lax.rem(d, side), lax.div(d, side)
    p = (1 - m) * x + m * y
    q = (1 - m) * y + m * x
    rows = weight.shape[0]
    count = tokens.shape[0]
    heads = kv.shape[0]
    per_half = side * side // 2
    z_parts = z_send.shape[0] - 3
    far = side // 2

    def wrap(i):
        return lax.rem(i + side, side)

    def spot(p_, q_):
        return (g, (1 - m) * (q_ * side + p_) + m * (p_ * side + q_), m)

    one_next = (spot(wrap(p + 1), q), spot(wrap(p - 1), q))
    two_next = (spot(p, wrap(q + 1)), spot(p, wrap(q - 1)))
    sibling = (g, d, 1 - m)
    partner = (g + 1 - 2 * lax.rem(g, 2), d, m)

    def block(c, k):
        return w_all.at[c, pl.ds(pl.multiple_of(k * rows, rows), rows)]

    def reach(r, way):
        return far if (r + way) % 2 == 0 else far - 1

    def one_copy(way, s, source=None):
        k = wrap(p - s) if way == PLUS else wrap(p + s)
        return remote(block(q, k), block(q, k), one_send.at[way, s - 1],
                      one_recv.at[way, s - 1], one_next[way])

    def one_start(way, s):
        k = wrap(p - s + 1) if way == PLUS else wrap(p + s - 1)
        source = weight if s == 1 else block(q, k)
        remote(source, block(q, k), one_send.at[way, s - 1],
               one_recv.at[way, s - 1], one_next[way]).start()

    def two_copy(r, way, s):
        c = wrap(q - s) if way == PLUS else wrap(q + s)
        k = wrap(p + r)
        return remote(block(c, k), block(c, k), two_send.at[r, way, s - 1],
                      two_recv.at[r, way, s - 1], two_next[way])

    def two_start(r, way, s):
        c = wrap(q - s + 1) if way == PLUS else wrap(q + s - 1)
        k = wrap(p + r)
        source = weight if (r == 0 and isinstance(s, int) and s == 1) else block(c, k)
        remote(source, block(c, k), two_send.at[r, way, s - 1],
               two_recv.at[r, way, s - 1], two_next[way]).start()

    def token_chunk(part, c):
        pieces = []
        for k in range(side):
            at = (1 - m) * (side * c + k) + m * (side * k + c)
            lanes = pl.ds(pl.multiple_of(lax.rem(at, per_half) * rows, rows), rows)
            pieces.append(tok[part, lax.div(at, per_half), :, lanes])
        return jnp.concatenate(pieces, axis=1)

    def add_chunk(c):
        acc[0] += jnp.dot(token_chunk(0, c), w_all[c], preferred_element_type=jnp.float32)

    z_rows = count // z_parts

    def z_part(i):
        return (pl.ds(i * z_rows, z_rows),)

    def z_tokens(i):
        at = pl.ds(i * z_rows, z_rows)
        return remote(tokens.at[at], tok.at[1, m, at], z_send.at[i], z_recv.at[i], partner)

    def pass_tokens(i):
        at = pl.ds(i * z_rows, z_rows)
        return remote(tok.at[1, m, at], tok.at[1, m, at], sib_send.at[1 + i],
                      sib_recv.at[1 + i], sibling)

    def sibling_tokens(i):
        at = pl.ds(i * z_rows, z_rows)
        return remote(tok.at[1, 1 - m, at], tok.at[1, 1 - m, at], sib_send.at[1 + i],
                      sib_recv.at[1 + i], sibling)

    own_weight = pltpu.make_async_copy(weight, block(q, p), local_sem.at[0])
    own_tokens = pltpu.make_async_copy(tokens, tok.at[0, m], local_sem.at[1])
    own_weight.start()
    own_tokens.start()
    meet(one_next + two_next + (sibling, partner))
    for way in (PLUS, MINUS):
        one_start(way, 1)
        two_start(0, way, 1)
    z_table = remote(table, tab, z_send.at[z_parts], z_recv.at[z_parts], partner)
    z_table.start()
    for i in range(z_parts):
        z_tokens(i).start()
    half_tokens = remote(tokens, tok.at[0, m], sib_send.at[0], sib_recv.at[0], sibling)
    half_tokens.start()
    acc[...] = jnp.zeros_like(acc)

    for s in range(1, far + 1):
        for way in (PLUS, MINUS):
            if s > (far if way == PLUS else far - 1):
                continue
            one_copy(way, s).wait_recv()
            if s < (far if way == PLUS else far - 1):
                one_start(way, s + 1)
            r = (-s) % side if way == PLUS else s
            for second in (PLUS, MINUS):
                two_start(r, second, 1)
    own_weight.wait()
    own_tokens.wait()
    remote(tok.at[0, 1 - m], tok.at[0, 1 - m], sib_send.at[0], sib_recv.at[0], sibling).wait_recv()

    order = [0]
    for s in range(1, far + 1):
        order += [(-s) % side] if s == far else [(-s) % side, s]

    def step(s, last):
        for r in order:
            for way in (PLUS, MINUS):
                if last:
                    if reach(r, way) == far:
                        two_copy(r, way, s).wait_recv()
                    continue
                two_copy(r, way, s).wait_recv()
                if reach(r, way) == far:
                    two_start(r, way, s + 1)
                else:
                    @pl.when(s < far - 1)
                    def _():
                        two_start(r, way, s + 1)

    add_chunk(q)

    @pl.loop(1, far)
    def _(s):
        step(s, False)
        z_tokens(s - 1).wait_recv()
        pass_tokens(s - 1).start()
        add_chunk(wrap(q - s))
        add_chunk(wrap(q + s))

    step(far, True)
    z_tokens(far - 1).wait_recv()
    pass_tokens(far - 1).start()
    for i in range(z_parts):
        sibling_tokens(i).wait_recv()
    z_table.wait_recv()

    even = lax.rem(g, 2) == 0
    plain = jnp.where(lax.broadcasted_iota(jnp.int32, tab.shape, 1) < DH // 2, 1.0, 0.0)
    span = acc.shape[2] // 2
    per_span = heads // 2

    def result(part, head, angles):
        return turned(acc[part, :, head * DH:(head + 1) * DH], angles).astype(jnp.bfloat16)

    def z_result(half):
        at = pl.ds(half * per_span, per_span)
        return remote(give.at[at], got.at[at], z_send.at[z_parts + 1 + half],
                      z_recv.at[z_parts + 1 + half], partner)

    theirs = jnp.where(even, tab[...], plain)
    for half in range(2):
        lanes = slice(half * span, (half + 1) * span)

        @pl.loop(0, side)
        def _(c):
            acc[1, :, lanes] += jnp.dot(
                token_chunk(1, c), w_all[c, :, lanes], preferred_element_type=jnp.float32
            )

        for head in range(half * per_span, (half + 1) * per_span):
            give[head] = result(1, head, theirs)
        z_result(half).start()
    add_chunk(wrap(q + far))
    ours = jnp.where(even, table[...], plain)
    mine = [result(0, head, ours) for head in range(heads)]
    for half in range(2):
        z_result(half).wait_recv()
        for head in range(half * per_span, (half + 1) * per_span):
            kv[head, :, :DH] = jnp.where(even, mine[head], got[head])
            kv[head, :, DH:] = jnp.where(even, got[head], mine[head])

    for way in (PLUS, MINUS):
        for s in range(1, far + 1 - way):
            one_copy(way, s).wait_send()
        for r in range(side):
            for s in range(1, reach(r, way) + 1):
                two_copy(r, way, s).wait_send()
    half_tokens.wait_send()
    z_table.wait_send()
    for i in range(z_parts):
        z_tokens(i).wait_send()
        pass_tokens(i).wait_send()
    for half in range(2):
        z_result(half).wait_send()


def attend_kernel(
    side, kv, queries, start, out, line, below, bias, local_sem,
    ring_send, ring_recv, up_send, up_recv,
):
    g, d, m = lax.axis_index("groups"), lax.axis_index("dp"), lax.axis_index("mp")
    x, y = lax.rem(d, side), lax.div(d, side)
    heads, count = kv.shape[0], kv.shape[1]
    group = queries.shape[1] // DH // heads
    far = side // 2
    half_row = far * count
    is_second = x < far

    def wrap(i):
        return lax.rem(i + side, side)

    ring = ((g, y * side + wrap(x + 1), m), (g, y * side + wrap(x - 1), m))
    above = (g, wrap(y + 1) * side + x, m)
    under = (g, wrap(y - 1) * side + x, m)

    def slot(h, at):
        return line.at[h, pl.ds(pl.multiple_of(at * count, count), count)]

    def up_slot(h, at):
        return below.at[h, pl.ds(pl.multiple_of(at * count, count), count)]

    def ring_copy(h, way, s):
        at = wrap(x - s) if way == PLUS else wrap(x + s)
        return remote(slot(h, at), slot(h, at), ring_send.at[h, way, s - 1],
                      ring_recv.at[h, way, s - 1], ring[way])

    def ring_start(h, way, s):
        at = wrap(x - s + 1) if way == PLUS else wrap(x + s - 1)
        remote(slot(h, at), slot(h, at), ring_send.at[h, way, s - 1],
               ring_recv.at[h, way, s - 1], ring[way]).start()

    def own_start(h):
        for way in (PLUS, MINUS):
            remote(kv.at[h], slot(h, x), ring_send.at[h, way, 0],
                   ring_recv.at[h, way, 0], ring[way]).start()

    def up_copy(h, at):
        return remote(slot(h, at + far), up_slot(h, at), up_send.at[h, at],
                      up_recv.at[h, at], above)

    def event(h, s):
        for way in (PLUS, MINUS):
            long_way = lax.rem(h + way, 2) == 0
            at = wrap(x - s) if way == PLUS else wrap(x + s)

            @pl.when((s < far) | long_way)
            def _():
                ring_copy(h, way, s).wait_recv()

                @pl.when((s < far - 1) | ((s == far - 1) & long_way))
                def _():
                    ring_start(h, way, s + 1)

                @pl.when(is_second & (at >= far))
                def _():
                    up_copy(h, at - far).start()

    own = [pltpu.make_async_copy(kv.at[h], slot(h, x), local_sem.at[h]) for h in range(heads)]
    for copy in own:
        copy.start()
    meet(ring + (above, under))
    own_start(0)
    own_start(1)

    @pl.when(jnp.logical_not(is_second))
    def _():
        below[...] = jnp.zeros_like(below)

    place = half_row + lax.rem(x, far) * count
    row = lax.broadcasted_iota(jnp.int32, (count, DH), 0) + place
    lane = lax.broadcasted_iota(jnp.int32, (count, DH), 1)
    for j in range(2 * half_row // DH):
        key = lane + j * DH
        fits = (key >= start[...]) & (key <= row)
        bias[:, j * DH:(j + 1) * DH] = jnp.where(fits, 0.0, -1e30)
    for copy in own:
        copy.wait()

    factor = math.log2(math.e) / math.sqrt(DH)
    base = pl.multiple_of((1 - lax.div(x + far, side)) * 0 + lax.div(x, far) * half_row, half_row)
    sub = 128
    contract = (((1,), (1,)), ((), ()))

    def piece(h, i):
        lanes = pl.ds(pl.multiple_of((h * group + i) * DH, DH), DH)
        for b in range(count // sub):
            at = slice(b * sub, (b + 1) * sub)
            q = queries[at, lanes]
            first = lax.dot_general(q, below[h, :, :DH], contract,
                                    preferred_element_type=jnp.float32) + bias[at, :half_row]
            second = lax.dot_general(q, line[h, pl.ds(base, half_row), :DH], contract,
                                     preferred_element_type=jnp.float32) + bias[at, half_row:]
            peak = jnp.maximum(jnp.max(first, axis=1, keepdims=True),
                               jnp.max(second, axis=1, keepdims=True))
            first = jnp.exp2((first - peak) * factor)
            second = jnp.exp2((second - peak) * factor)
            total = jnp.sum(first, axis=1, keepdims=True) + jnp.sum(second, axis=1, keepdims=True)
            scale = 1.0 / total
            mixed = jnp.dot((first * scale).astype(jnp.bfloat16), below[h, :, DH:],
                            preferred_element_type=jnp.float32)
            mixed += jnp.dot((second * scale).astype(jnp.bfloat16),
                             line[h, pl.ds(base, half_row), DH:],
                             preferred_element_type=jnp.float32)
            out[at, lanes] = mixed.astype(jnp.bfloat16)

    lag = far + 1
    units = group // 2

    @pl.loop(1, 2 * heads + lag)
    def _(k):
        h_one = lax.div(k - 1, 2)
        s_one = 1 + lax.rem(k - 1, 2)
        h_two, s_two = h_one - 1, s_one + 2

        @pl.when((s_one == 1) & (h_one >= 1) & (h_one + 1 < heads))
        def _():
            own_start(h_one + 1)

        @pl.when((h_two >= 0) & (h_two < heads))
        def _():
            event(h_two, s_two)

        @pl.when(h_one < heads)
        def _():
            event(h_one, s_one)

        @pl.when(k >= lag)
        def _():
            h = lax.div(k - lag, 2)

            @pl.when((lax.rem(k - lag, 2) == 0) & is_second)
            def _():
                for at in range(far):
                    up_copy(h, at).wait_recv()

            @pl.loop(0, units)
            def _(i):
                piece(h, lax.rem(k - lag, 2) * units + i)

    @pl.loop(0, heads)
    def _(h):
        for way in (PLUS, MINUS):
            for s in range(1, far):
                ring_copy(h, way, s).wait_send()

            @pl.when(lax.rem(h + way, 2) == 0)
            def _():
                ring_copy(h, way, far).wait_send()

        @pl.when(is_second)
        def _():
            for at in range(far):
                up_copy(h, at).wait_send()


def per_device(side, tokens, queries, w_key, w_value, lengths):
    count, wide = tokens.shape
    columns = w_key.shape[1]
    heads = columns // DH
    far = side // 2
    half_row = ROW // 2
    g, d = lax.axis_index("groups"), lax.axis_index("dp")

    all_tokens = count * side * side
    first_token = (d * count - half_row + all_tokens) % all_tokens
    row_index = first_token // ROW
    row_lengths = lax.dynamic_slice_in_dim(lengths, row_index, 1, 0)[0]
    finish = jnp.cumsum(row_lengths)
    offsets = first_token - row_index * ROW + jnp.arange(count, dtype=jnp.int32)
    before = finish[None, :] <= offsets[:, None]
    started = jnp.sum(jnp.where(before, row_lengths[None, :], 0), axis=1)
    positions = (offsets - started).astype(jnp.float32)
    frequency = jnp.power(
        500000.0, -2.0 * jnp.arange(DH // 2, dtype=jnp.float32) / DH
    )
    angles = positions[:, None] * frequency[None, :]
    table = jnp.concatenate([jnp.cos(angles), jnp.sin(angles)], axis=1)
    shift = jnp.where(d % side >= far, half_row, 0)
    start = jnp.broadcast_to((started + shift)[:, None], (count, DH))
    weight = jnp.where(g % 2 == 0, w_key, w_value)

    vmem = pl.BlockSpec(memory_space=pltpu.VMEM)
    hbm = pl.BlockSpec(memory_space=pl.ANY)
    dma = pltpu.SemaphoreType.DMA
    rows = weight.shape[0]
    z_parts = far
    kv = pl.pallas_call(
        functools.partial(project_kernel, side),
        out_shape=jax.ShapeDtypeStruct((heads, count, 2 * DH), jnp.bfloat16),
        in_specs=[hbm, hbm, vmem],
        out_specs=vmem,
        scratch_shapes=[
            pltpu.VMEM((2, 2, count, wide), jnp.bfloat16),
            pltpu.VMEM((side, side * rows, columns), jnp.bfloat16),
            pltpu.VMEM((count, DH), jnp.float32),
            pltpu.VMEM((2, count, columns), jnp.float32),
            pltpu.VMEM((heads, count, DH), jnp.bfloat16),
            pltpu.VMEM((heads, count, DH), jnp.bfloat16),
            dma((2,)),
            dma((2, far)),
            dma((2, far)),
            dma((side, 2, far)),
            dma((side, 2, far)),
            dma((1 + z_parts,)),
            dma((1 + z_parts,)),
            dma((z_parts + 3,)),
            dma((z_parts + 3,)),
        ],
        compiler_params=pltpu.CompilerParams(collective_id=0, has_side_effects=True),
        name="project",
    )(tokens, weight, table)
    return pl.pallas_call(
        functools.partial(attend_kernel, side),
        out_shape=jax.ShapeDtypeStruct(queries.shape, jnp.bfloat16),
        in_specs=[hbm, vmem, vmem],
        out_specs=vmem,
        scratch_shapes=[
            pltpu.VMEM((heads, side * count, 2 * DH), jnp.bfloat16),
            pltpu.VMEM((heads, far * count, 2 * DH), jnp.bfloat16),
            pltpu.VMEM((count, 2 * half_row), jnp.float32),
            dma((heads,)),
            dma((heads, 2, far)),
            dma((heads, 2, far)),
            dma((heads, far)),
            dma((heads, far)),
        ],
        compiler_params=pltpu.CompilerParams(collective_id=1, has_side_effects=True),
        name="attend",
    )(kv, queries, start)


def solution(mesh):
    side = math.isqrt(mesh.shape["dp"])
    return jax.shard_map(
        functools.partial(per_device, side),
        mesh=mesh,
        in_specs=(
            P(("groups", "dp"), "mp"),
            P(("groups", "dp"), "mp"),
            P("dp", "mp"),
            P("dp", "mp"),
            P("groups", None),
        ),
        out_specs=P(("groups", "dp"), "mp"),
        check_vma=False,
    )
```

```python
import functools
import math

import jax
import jax.numpy as jnp
from jax import lax
from jax.experimental import pallas as pl
from jax.experimental.pallas import tpu as pltpu
from jax.sharding import PartitionSpec as P

DH = 128
ROW = 2048
MESH = pl.DeviceIdType.MESH
PLUS, MINUS = 0, 1


def remote(src, dst, send, recv, device):
    return pltpu.make_async_remote_copy(
        src_ref=src,
        dst_ref=dst,
        send_sem=send,
        recv_sem=recv,
        device_id=device,
        device_id_type=MESH,
    )


def meet(neighbours):
    barrier = pltpu.get_barrier_semaphore()
    for device in neighbours:
        pl.semaphore_signal(barrier, inc=1, device_id=device, device_id_type=MESH)
    pl.semaphore_wait(barrier, len(neighbours))


def turned(x, table):
    half = DH // 2
    lane = lax.broadcasted_iota(jnp.int32, table.shape, 1)
    other = pltpu.roll(table, half, 1)
    cosine = jnp.where(lane < half, table, other)
    sine = jnp.where(lane < half, -other, table)
    return x * cosine + pltpu.roll(x, half, 1) * sine


def project_kernel(
    side, tokens, weight, table, kv, tok, w_all, tab, acc, give, got, local_sem,
    one_send, one_recv, two_send, two_recv, sib_send, sib_recv, z_send, z_recv,
):
    g, d, m = lax.axis_index("groups"), lax.axis_index("dp"), lax.axis_index("mp")
    x, y = lax.rem(d, side), lax.div(d, side)
    p = (1 - m) * x + m * y
    q = (1 - m) * y + m * x
    rows = weight.shape[0]
    count = tokens.shape[0]
    heads = kv.shape[0]
    per_half = side * side // 2
    z_parts = z_send.shape[0] - 3
    far = side // 2

    def wrap(i):
        return lax.rem(i + side, side)

    def spot(p_, q_):
        return (g, (1 - m) * (q_ * side + p_) + m * (p_ * side + q_), m)

    one_next = (spot(wrap(p + 1), q), spot(wrap(p - 1), q))
    two_next = (spot(p, wrap(q + 1)), spot(p, wrap(q - 1)))
    sibling = (g, d, 1 - m)
    partner = (g + 1 - 2 * lax.rem(g, 2), d, m)

    def block(c, k):
        return w_all.at[c, pl.ds(pl.multiple_of(k * rows, rows), rows)]

    def reach(r, way):
        return far if (r + way) % 2 == 0 else far - 1

    def one_copy(way, s, source=None):
        k = wrap(p - s) if way == PLUS else wrap(p + s)
        return remote(block(q, k), block(q, k), one_send.at[way, s - 1],
                      one_recv.at[way, s - 1], one_next[way])

    def one_start(way, s):
        k = wrap(p - s + 1) if way == PLUS else wrap(p + s - 1)
        source = weight if s == 1 else block(q, k)
        remote(source, block(q, k), one_send.at[way, s - 1],
               one_recv.at[way, s - 1], one_next[way]).start()

    def two_copy(r, way, s):
        c = wrap(q - s) if way == PLUS else wrap(q + s)
        k = wrap(p + r)
        return remote(block(c, k), block(c, k), two_send.at[r, way, s - 1],
                      two_recv.at[r, way, s - 1], two_next[way])

    def two_start(r, way, s):
        c = wrap(q - s + 1) if way == PLUS else wrap(q + s - 1)
        k = wrap(p + r)
        source = weight if (r == 0 and isinstance(s, int) and s == 1) else block(c, k)
        remote(source, block(c, k), two_send.at[r, way, s - 1],
               two_recv.at[r, way, s - 1], two_next[way]).start()

    def token_chunk(part, c):
        pieces = []
        for k in range(side):
            at = (1 - m) * (side * c + k) + m * (side * k + c)
            lanes = pl.ds(pl.multiple_of(lax.rem(at, per_half) * rows, rows), rows)
            pieces.append(tok[part, lax.div(at, per_half), :, lanes])
        return jnp.concatenate(pieces, axis=1)

    def add_chunk(c):
        acc[0] += jnp.dot(token_chunk(0, c), w_all[c], preferred_element_type=jnp.float32)

    z_rows = count // z_parts

    def z_part(i):
        return (pl.ds(i * z_rows, z_rows),)

    def z_tokens(i):
        at = pl.ds(i * z_rows, z_rows)
        return remote(tokens.at[at], tok.at[1, m, at], z_send.at[i], z_recv.at[i], partner)

    def pass_tokens(i):
        at = pl.ds(i * z_rows, z_rows)
        return remote(tok.at[1, m, at], tok.at[1, m, at], sib_send.at[1 + i],
                      sib_recv.at[1 + i], sibling)

    def sibling_tokens(i):
        at = pl.ds(i * z_rows, z_rows)
        return remote(tok.at[1, 1 - m, at], tok.at[1, 1 - m, at], sib_send.at[1 + i],
                      sib_recv.at[1 + i], sibling)

    own_weight = pltpu.make_async_copy(weight, block(q, p), local_sem.at[0])
    own_tokens = pltpu.make_async_copy(tokens, tok.at[0, m], local_sem.at[1])
    own_weight.start()
    own_tokens.start()
    meet(one_next + two_next + (sibling, partner))
    for way in (PLUS, MINUS):
        one_start(way, 1)
        two_start(0, way, 1)
    z_table = remote(table, tab, z_send.at[z_parts], z_recv.at[z_parts], partner)
    z_table.start()
    for i in range(z_parts):
        z_tokens(i).start()
    half_tokens = remote(tokens, tok.at[0, m], sib_send.at[0], sib_recv.at[0], sibling)
    half_tokens.start()
    acc[...] = jnp.zeros_like(acc)

    for s in range(1, far + 1):
        for way in (PLUS, MINUS):
            if s > (far if way == PLUS else far - 1):
                continue
            one_copy(way, s).wait_recv()
            if s < (far if way == PLUS else far - 1):
                one_start(way, s + 1)
            r = (-s) % side if way == PLUS else s
            for second in (PLUS, MINUS):
                two_start(r, second, 1)
    own_weight.wait()
    own_tokens.wait()
    remote(tok.at[0, 1 - m], tok.at[0, 1 - m], sib_send.at[0], sib_recv.at[0], sibling).wait_recv()

    order = [0]
    for s in range(1, far + 1):
        order += [(-s) % side] if s == far else [(-s) % side, s]

    def step(s, last):
        for r in order:
            for way in (PLUS, MINUS):
                if last:
                    if reach(r, way) == far:
                        two_copy(r, way, s).wait_recv()
                    continue
                two_copy(r, way, s).wait_recv()
                if reach(r, way) == far:
                    two_start(r, way, s + 1)
                else:
                    @pl.when(s < far - 1)
                    def _():
                        two_start(r, way, s + 1)

    add_chunk(q)

    @pl.loop(1, far)
    def _(s):
        step(s, False)
        z_tokens(s - 1).wait_recv()
        pass_tokens(s - 1).start()
        add_chunk(wrap(q - s))
        add_chunk(wrap(q + s))

    step(far, True)
    z_tokens(far - 1).wait_recv()
    pass_tokens(far - 1).start()
    for i in range(z_parts):
        sibling_tokens(i).wait_recv()
    z_table.wait_recv()

    even = lax.rem(g, 2) == 0
    plain = jnp.where(lax.broadcasted_iota(jnp.int32, tab.shape, 1) < DH // 2, 1.0, 0.0)
    span = acc.shape[2] // 2
    per_span = heads // 2

    def result(part, head, angles):
        return turned(acc[part, :, head * DH:(head + 1) * DH], angles).astype(jnp.bfloat16)

    def z_result(half):
        at = pl.ds(half * per_span, per_span)
        return remote(give.at[at], got.at[at], z_send.at[z_parts + 1 + half],
                      z_recv.at[z_parts + 1 + half], partner)

    theirs = jnp.where(even, tab[...], plain)
    for half in range(2):
        lanes = slice(half * span, (half + 1) * span)

        @pl.loop(0, side)
        def _(c):
            acc[1, :, lanes] += jnp.dot(
                token_chunk(1, c), w_all[c, :, lanes], preferred_element_type=jnp.float32
            )

        for head in range(half * per_span, (half + 1) * per_span):
            give[head] = result(1, head, theirs)
        z_result(half).start()
    add_chunk(wrap(q + far))
    ours = jnp.where(even, table[...], plain)
    mine = [result(0, head, ours) for head in range(heads)]
    for half in range(2):
        z_result(half).wait_recv()
        for head in range(half * per_span, (half + 1) * per_span):
            kv[head, :, :DH] = jnp.where(even, mine[head], got[head])
            kv[head, :, DH:] = jnp.where(even, got[head], mine[head])

    for way in (PLUS, MINUS):
        for s in range(1, far + 1 - way):
            one_copy(way, s).wait_send()
        for r in range(side):
            for s in range(1, reach(r, way) + 1):
                two_copy(r, way, s).wait_send()
    half_tokens.wait_send()
    z_table.wait_send()
    for i in range(z_parts):
        z_tokens(i).wait_send()
        pass_tokens(i).wait_send()
    for half in range(2):
        z_result(half).wait_send()


def attend_kernel(
    side, kv, queries, start, out, line, below, bias, score_a, score_b, peak_a, peak_b,
    weight_a, weight_b, total_a, total_b, local_sem, ring_send, ring_recv, up_send, up_recv,
):
    scores, peaks = (score_a, score_b), (peak_a, peak_b)
    weights, totals = (weight_a, weight_b), (total_a, total_b)
    g, d, m = lax.axis_index("groups"), lax.axis_index("dp"), lax.axis_index("mp")
    x, y = lax.rem(d, side), lax.div(d, side)
    heads, count = kv.shape[0], kv.shape[1]
    group = queries.shape[1] // DH // heads
    far = side // 2
    half_row = far * count
    is_second = x < far

    def wrap(i):
        return lax.rem(i + side, side)

    ring = ((g, y * side + wrap(x + 1), m), (g, y * side + wrap(x - 1), m))
    above = (g, wrap(y + 1) * side + x, m)
    under = (g, wrap(y - 1) * side + x, m)

    def slot(h, at):
        return line.at[h, pl.ds(pl.multiple_of(at * count, count), count)]

    def up_slot(h, at):
        return below.at[h, pl.ds(pl.multiple_of(at * count, count), count)]

    def ring_copy(h, way, s):
        at = wrap(x - s) if way == PLUS else wrap(x + s)
        return remote(slot(h, at), slot(h, at), ring_send.at[h, way, s - 1],
                      ring_recv.at[h, way, s - 1], ring[way])

    def ring_start(h, way, s):
        at = wrap(x - s + 1) if way == PLUS else wrap(x + s - 1)
        remote(slot(h, at), slot(h, at), ring_send.at[h, way, s - 1],
               ring_recv.at[h, way, s - 1], ring[way]).start()

    def own_start(h):
        for way in (PLUS, MINUS):
            remote(kv.at[h], slot(h, x), ring_send.at[h, way, 0],
                   ring_recv.at[h, way, 0], ring[way]).start()

    def up_copy(h, at):
        return remote(slot(h, at + far), up_slot(h, at), up_send.at[h, at],
                      up_recv.at[h, at], above)

    def event(h, s):
        for way in (PLUS, MINUS):
            long_way = lax.rem(h + way, 2) == 0
            at = wrap(x - s) if way == PLUS else wrap(x + s)

            @pl.when((s < far) | long_way)
            def _():
                ring_copy(h, way, s).wait_recv()

                @pl.when((s < far - 1) | ((s == far - 1) & long_way))
                def _():
                    ring_start(h, way, s + 1)

                @pl.when(is_second & (at >= far))
                def _():
                    up_copy(h, at - far).start()

    own = [pltpu.make_async_copy(kv.at[h], slot(h, x), local_sem.at[h]) for h in range(heads)]
    for copy in own:
        copy.start()
    meet(ring + (above, under))
    own_start(0)
    own_start(1)

    @pl.when(jnp.logical_not(is_second))
    def _():
        below[...] = jnp.zeros_like(below)

    place = half_row + lax.rem(x, far) * count
    row = lax.broadcasted_iota(jnp.int32, (count, DH), 0) + place
    lane = lax.broadcasted_iota(jnp.int32, (count, DH), 1)
    for j in range(2 * half_row // DH):
        key = lane + j * DH
        fits = (key >= start[...]) & (key <= row)
        bias[:, j * DH:(j + 1) * DH] = jnp.where(fits, 0.0, -1e30)
    for copy in own:
        copy.wait()

    factor = math.log2(math.e) / math.sqrt(DH)
    base = pl.multiple_of((1 - lax.div(x + far, side)) * 0 + lax.div(x, far) * half_row, half_row)
    contract = (((1,), (1,)), ((), ()))
    keys = 2 * half_row
    wide, tall = 512, 64

    def key_rows(j):
        if j < half_row:
            return below, pl.ds(j, wide)
        return line, pl.ds(pl.multiple_of(base + j - half_row, wide), wide)

    def lanes_of(t):
        return pl.ds(pl.multiple_of(t * DH, DH), DH)

    def score(t, into):
        h = lax.div(t, group)
        q = queries[:, lanes_of(t)]
        peak = None
        for j in range(0, keys, wide):
            ref, rows = key_rows(j)
            s = lax.dot_general(q, ref[h, rows, :DH], contract,
                                preferred_element_type=jnp.float32) + bias[:, j:j + wide]
            scores[into][:, j:j + wide] = s
            for b in range(0, wide, DH):
                part = s[:, b:b + DH]
                peak = part if peak is None else jnp.maximum(peak, part)
        peaks[into][...] = peak

    def weigh(into):
        for r in range(0, count, tall):
            at = slice(r, r + tall)
            peak = jnp.max(peaks[into][at], axis=1, keepdims=True)
            total = jnp.zeros((tall, DH), jnp.float32)
            for j in range(0, keys, 2 * DH):
                e = jnp.exp2((scores[into][at, j:j + 2 * DH] - peak) * factor)
                total += e[:, :DH] + e[:, DH:]
                weights[into][at, j:j + 2 * DH] = e.astype(jnp.bfloat16)
            totals[into][at] = total

    def mix(t, into):
        h = lax.div(t, group)
        mixed = None
        for j in range(0, keys, half_row):
            ref = below if j < half_row else line
            rows = pl.ds(0, half_row) if j < half_row else pl.ds(base, half_row)
            part = jnp.dot(weights[into][:, j:j + half_row], ref[h, rows, DH:],
                           preferred_element_type=jnp.float32)
            mixed = part if mixed is None else mixed + part
        total = jnp.sum(totals[into][...], axis=1, keepdims=True)
        out[:, lanes_of(t)] = (mixed / total).astype(jnp.bfloat16)

    def pair(t):
        last = lax.rem(t, group) == group - 2
        score(t + 1, 1)
        weigh(0)
        mix(jnp.maximum(t - 1, 0), 1)
        score(jnp.where(last, t, t + 2), 0)
        weigh(1)
        mix(t, 0)

    lag = far + 1
    units = group // 2

    @pl.loop(1, 2 * heads + lag)
    def _(k):
        h_one = lax.div(k - 1, 2)
        s_one = 1 + lax.rem(k - 1, 2)
        h_two, s_two = h_one - 1, s_one + 2

        @pl.when((s_one == 1) & (h_one >= 1) & (h_one + 1 < heads))
        def _():
            own_start(h_one + 1)

        @pl.when((h_two >= 0) & (h_two < heads))
        def _():
            event(h_two, s_two)

        @pl.when(h_one < heads)
        def _():
            event(h_one, s_one)

        @pl.when(k >= lag)
        def _():
            h = lax.div(k - lag, 2)

            @pl.when((lax.rem(k - lag, 2) == 0) & is_second)
            def _():
                for at in range(far):
                    up_copy(h, at).wait_recv()

            @pl.when(lax.rem(k - lag, 2) == 0)
            def _():
                score(h * group, 0)

            @pl.loop(0, units // 2)
            def _(i):
                pair((k - lag) * units + 2 * i)

    mix(heads * group - 1, 1)

    @pl.loop(0, heads)
    def _(h):
        for way in (PLUS, MINUS):
            for s in range(1, far):
                ring_copy(h, way, s).wait_send()

            @pl.when(lax.rem(h + way, 2) == 0)
            def _():
                ring_copy(h, way, far).wait_send()

        @pl.when(is_second)
        def _():
            for at in range(far):
                up_copy(h, at).wait_send()


def per_device(side, tokens, queries, w_key, w_value, lengths):
    count, wide = tokens.shape
    columns = w_key.shape[1]
    heads = columns // DH
    far = side // 2
    half_row = ROW // 2
    g, d = lax.axis_index("groups"), lax.axis_index("dp")

    all_tokens = count * side * side
    first_token = (d * count - half_row + all_tokens) % all_tokens
    row_index = first_token // ROW
    row_lengths = lax.dynamic_slice_in_dim(lengths, row_index, 1, 0)[0]
    finish = jnp.cumsum(row_lengths)
    offsets = first_token - row_index * ROW + jnp.arange(count, dtype=jnp.int32)
    before = finish[None, :] <= offsets[:, None]
    started = jnp.sum(jnp.where(before, row_lengths[None, :], 0), axis=1)
    positions = (offsets - started).astype(jnp.float32)
    frequency = jnp.power(
        500000.0, -2.0 * jnp.arange(DH // 2, dtype=jnp.float32) / DH
    )
    angles = positions[:, None] * frequency[None, :]
    table = jnp.concatenate([jnp.cos(angles), jnp.sin(angles)], axis=1)
    shift = jnp.where(d % side >= far, half_row, 0)
    start = jnp.broadcast_to((started + shift)[:, None], (count, DH))
    weight = jnp.where(g % 2 == 0, w_key, w_value)

    vmem = pl.BlockSpec(memory_space=pltpu.VMEM)
    hbm = pl.BlockSpec(memory_space=pl.ANY)
    dma = pltpu.SemaphoreType.DMA
    rows = weight.shape[0]
    z_parts = far
    kv = pl.pallas_call(
        functools.partial(project_kernel, side),
        out_shape=jax.ShapeDtypeStruct((heads, count, 2 * DH), jnp.bfloat16),
        in_specs=[hbm, hbm, vmem],
        out_specs=vmem,
        scratch_shapes=[
            pltpu.VMEM((2, 2, count, wide), jnp.bfloat16),
            pltpu.VMEM((side, side * rows, columns), jnp.bfloat16),
            pltpu.VMEM((count, DH), jnp.float32),
            pltpu.VMEM((2, count, columns), jnp.float32),
            pltpu.VMEM((heads, count, DH), jnp.bfloat16),
            pltpu.VMEM((heads, count, DH), jnp.bfloat16),
            dma((2,)),
            dma((2, far)),
            dma((2, far)),
            dma((side, 2, far)),
            dma((side, 2, far)),
            dma((1 + z_parts,)),
            dma((1 + z_parts,)),
            dma((z_parts + 3,)),
            dma((z_parts + 3,)),
        ],
        compiler_params=pltpu.CompilerParams(collective_id=0, has_side_effects=True),
        name="project",
    )(tokens, weight, table)
    return pl.pallas_call(
        functools.partial(attend_kernel, side),
        out_shape=jax.ShapeDtypeStruct(queries.shape, jnp.bfloat16),
        in_specs=[hbm, vmem, vmem],
        out_specs=vmem,
        scratch_shapes=[
            pltpu.VMEM((heads, side * count, 2 * DH), jnp.bfloat16),
            pltpu.VMEM((heads, far * count, 2 * DH), jnp.bfloat16),
            pltpu.VMEM((count, 2 * half_row), jnp.float32),
            pltpu.VMEM((count, 2 * half_row), jnp.float32),
            pltpu.VMEM((count, 2 * half_row), jnp.float32),
            pltpu.VMEM((count, DH), jnp.float32),
            pltpu.VMEM((count, DH), jnp.float32),
            pltpu.VMEM((count, 2 * half_row), jnp.bfloat16),
            pltpu.VMEM((count, 2 * half_row), jnp.bfloat16),
            pltpu.VMEM((count, DH), jnp.float32),
            pltpu.VMEM((count, DH), jnp.float32),
            dma((heads,)),
            dma((heads, 2, far)),
            dma((heads, 2, far)),
            dma((heads, far)),
            dma((heads, far)),
        ],
        compiler_params=pltpu.CompilerParams(collective_id=1, has_side_effects=True),
        name="attend",
    )(kv, queries, start)


def solution(mesh):
    side = math.isqrt(mesh.shape["dp"])
    return jax.shard_map(
        functools.partial(per_device, side),
        mesh=mesh,
        in_specs=(
            P(("groups", "dp"), "mp"),
            P(("groups", "dp"), "mp"),
            P("dp", "mp"),
            P("dp", "mp"),
            P("groups", None),
        ),
        out_specs=P(("groups", "dp"), "mp"),
        check_vma=False,
    )
```
